128 devices in a mesh: ctx: 8 (over x, core), exp: 16 (over z, y).
Axes of the slice: x: 4, y: 4, z: 4, core: 2. Of those that a mesh axis runs over, the one named last changes fastest.
Arguments:
- hidden_in: bfloat16 [16, 1024, 2048], P('exp', 'ctx'), may hold values from -6 to 6
- grad_out: bfloat16 [16, 1024, 2048], P('exp', 'ctx'), may hold values from -6 to 6
- post_gain: float32 [2048], replicated, may hold values from 0.1 to 1.9
- route_ids: int32 [16, 1024, 10], P('exp', 'ctx'), may hold values from 0 to 511, as said below
- route_weight: float32 [16, 1024, 10], P('exp', 'ctx'), may hold values from 0.02 to 0.3
- gate_up: bfloat16 [128, 2048, 1024], P(('ctx', 'exp')), may hold values from -0.125 to 0.125
- down_proj: bfloat16 [128, 512, 2048], P(('ctx', 'exp')), may hold values from -0.25 to 0.25
- query_in: bfloat16 [16, 1024, 1024], P('exp', 'ctx'), may hold values from -6 to 6
- key_in: bfloat16 [16, 1024, 1024], P('exp', 'ctx'), may hold values from -6 to 6
- value_in: bfloat16 [16, 1024, 2048], P('exp', 'ctx'), may hold values from -6 to 6
- gate_in: bfloat16 [16, 1024, 2048], P('exp', 'ctx'), may hold values from -6 to 6
- decay_logit: bfloat16 [16, 1024, 16], P('exp', 'ctx'), may hold values from -12 to 0.5
- beta_logit: bfloat16 [16, 1024, 16], P('exp', 'ctx'), may hold values from -6 to 6
- head_gain: float32 [128], replicated, may hold values from 0.1 to 1.9
- out_proj: bfloat16 [2048, 2048], P(None, 'ctx'), may hold values from -0.125 to 0.125
Outputs:
- grad_hidden: bfloat16 [16, 1024, 2048], P('exp', 'ctx')
- grad_query: bfloat16 [16, 1024, 1024], P('exp', 'ctx')
- grad_key: bfloat16 [16, 1024, 1024], P('exp', 'ctx')
- grad_value: bfloat16 [16, 1024, 2048], P('exp', 'ctx')
- grad_gate: bfloat16 [16, 1024, 2048], P('exp', 'ctx')
- grad_decay: bfloat16 [16, 1024, 16], P('exp', 'ctx')
- grad_beta: bfloat16 [16, 1024, 16], P('exp', 'ctx')
- grad_gate_up: bfloat16 [128, 2048, 1024], P(('ctx', 'exp'))
- grad_down: bfloat16 [128, 512, 2048], P(('ctx', 'exp'))
- grad_out_proj: float32 [2048, 2048], P('exp', 'ctx')
The draws below stay inside these ranges and needn't reach their ends.
Inputs may be any that keep to these rules, and one draw needn't show every extreme that they name: `route_ids`: each token names 10 different experts. The 128 positions of a sequence on one device name no expert more than 4 times, and one expert below 128, the same on every device, is named exactly 4 times by them.
All inputs are finite; a program needn't handle non-finite values.
Results may differ from the reference program's by a relative error of at most 0.014.
Values may be sent and summed in bfloat16 or wider, within the bound.
No kernel may reach another device: no remote copies, remote signals or barrier semaphores. Data moves between devices by JAX's collectives and lax.ppermute only.
A program may use at most 128 MiB of HBM per device.

```python
import jax
import jax.numpy as jnp
from jax import lax

D = 2048
F = 512
EXPERTS = 512
EXPERTS_PER_TOKEN = 10
VH = 16
DK = 128
BLOCK = 128
DEVICE_TOKENS = 128
EXPERT_ROW_LIMIT = 4
HELD = 128
SEQUENCE_COUNT = 16
WINDOW_LENGTH = 1024
TOKENS = 16384
KD = 1024
VD = 2048


def draw_route_ids(key, part):
    block_total = SEQUENCE_COUNT * WINDOW_LENGTH // DEVICE_TOKENS
    hottest = jax.random.randint(jax.random.fold_in(key, 7), (), 0, HELD)

    def one_block(index):
        block_key = jax.random.fold_in(key, index)
        first, second, third_piece, fourth_piece = jax.random.split(block_key, 4)
        ordering = (hottest + 1 + jax.random.permutation(first, EXPERTS - 1)) % EXPERTS
        offset = jax.random.randint(second, (), 0, EXPERTS - 1)
        token_rows = jnp.arange(DEVICE_TOKENS)
        places = (offset + token_rows[:, None] * EXPERTS_PER_TOKEN + jnp.arange(EXPERTS_PER_TOKEN)[None, :]) % (EXPERTS - 1)
        chosen = ordering[places]
        holder_rows = jax.random.permutation(third_piece, DEVICE_TOKENS) < EXPERT_ROW_LIMIT
        chosen_slot_index = jax.random.randint(fourth_piece, (DEVICE_TOKENS,), 0, EXPERTS_PER_TOKEN)
        slot_assigned = holder_rows[:, None] & (jnp.arange(EXPERTS_PER_TOKEN)[None, :] == chosen_slot_index[:, None])
        return jnp.where(slot_assigned, hottest, chosen)
    every_block = jax.vmap(one_block)(jnp.arange(block_total))
    return every_block.reshape(SEQUENCE_COUNT, WINDOW_LENGTH, EXPERTS_PER_TOKEN).astype(jnp.int32)


def draw_decay_logit(key, part):
    first, second, third_piece, fourth_piece, fifth = jax.random.split(key, 5)
    quick = jax.random.uniform(first, (VH,)) < 0.5
    spread = jnp.exp(jax.random.uniform(second, (SEQUENCE_COUNT, 1, VH), minval=0.0, maxval=0.7))
    rough = jnp.exp(jax.random.uniform(third_piece, (SEQUENCE_COUNT, WINDOW_LENGTH, VH), minval=-0.7, maxval=0.7))
    base_rate = jnp.where(quick, 1.0 / 40.0, 0.3 / WINDOW_LENGTH)
    rates = base_rate * spread * rough
    spill_position = jax.random.randint(fourth_piece, (SEQUENCE_COUNT, 2), 0, WINDOW_LENGTH)
    spilling_over = jnp.any(jnp.arange(WINDOW_LENGTH)[None, :, None] == spill_position[:, None, :], axis=-1)
    losses = jax.random.uniform(fifth, (SEQUENCE_COUNT, WINDOW_LENGTH, VH), minval=0.2, maxval=0.5)
    rates = jnp.where(spilling_over[:, :, None], -jnp.log1p(-losses), rates)
    return jnp.log(jnp.expm1(rates)).astype(jnp.float32).astype(jnp.bfloat16)


def coherent_mask(key):
    picked = jax.random.randint(jax.random.fold_in(key, 70001), (SEQUENCE_COUNT,), 0, WINDOW_LENGTH // BLOCK)
    block_of = jnp.arange(WINDOW_LENGTH) // BLOCK
    return block_of[None, :] == picked[:, None]


def draw_key_in(key, part):
    first, second = jax.random.split(jax.random.fold_in(key, 70003))
    coherent = coherent_mask(key)[:, :, None]
    shape = (SEQUENCE_COUNT, WINDOW_LENGTH, KD)
    direction = jnp.where(jax.random.bernoulli(second, 0.5, (SEQUENCE_COUNT, 1, KD)), 1.0, -1.0)
    noise = jax.random.normal(first, shape)
    values = jnp.where(coherent, 4.0 * direction + noise, noise)
    return jnp.clip(values, -6.0, 6.0).astype(jnp.float32).astype(jnp.bfloat16)


def draw_beta_logit(key, part):
    first, second = jax.random.split(jax.random.fold_in(key, 70005))
    coherent = coherent_mask(key)[:, :, None]
    shape = (SEQUENCE_COUNT, WINDOW_LENGTH, VH)
    spread = 1.5 * jax.random.normal(first, shape)
    strong = 4.0 + 0.5 * jax.random.normal(second, shape)
    values = jnp.where(coherent, strong, spread)
    return jnp.clip(values, -6.0, 6.0).astype(jnp.float32).astype(jnp.bfloat16)


def steps_of(own_key, shape, shards, smallest, high):
    loudness, own = 1.0, jax.random.fold_in(own_key, 6)
    for dim, shards_of in shards:
        heights = jnp.exp(jax.random.uniform(jax.random.fold_in(own, dim), (shards_of,), jnp.float32, smallest / len(shards), high / len(shards)))
        loudness = loudness * jnp.repeat(heights, shape[dim] // shards_of).reshape([-1 if axis == dim else 1 for axis in range(len(shape))])
    return loudness


def scatter_about(rng, extent, scale, bound, cuts=(), kind=jnp.bfloat16):
    values = scale * jax.random.normal(rng, extent, jnp.float32)
    if cuts:
        values = values * steps_of(rng, extent, cuts, -0.22, 0.18)
    return jnp.clip(values, -bound, bound).astype(kind)


def setup_inputs(seed: int = 0) -> dict:
    key_of = jax.random.split(jax.random.key(seed), 16)
    return {
        "hidden_in": scatter_about(key_of[0], (SEQUENCE_COUNT, WINDOW_LENGTH, D), 1.0, 6.0, ((0, 16), (1, 8))),
        "grad_out": scatter_about(key_of[1], (SEQUENCE_COUNT, WINDOW_LENGTH, D), 1.0, 6.0, ((0, 16), (1, 8))),
        "post_gain": jnp.clip(1.0 + 0.18 * jax.random.normal(key_of[2], (D,), jnp.float32), 0.1, 1.9),
        "route_ids": draw_route_ids(jax.random.fold_in(key_of[15], 71), 0),
        "route_weight": jnp.clip(0.02 + 0.28 * jax.random.uniform(key_of[4], (SEQUENCE_COUNT, WINDOW_LENGTH, EXPERTS_PER_TOKEN), jnp.float32) ** steps_of(key_of[4], (SEQUENCE_COUNT, WINDOW_LENGTH, EXPERTS_PER_TOKEN), ((0, 16), (1, 8)), -0.2, 0.2), 0.02, 0.3),
        "gate_up": scatter_about(key_of[5], (HELD, D, 2 * F), D ** -0.5, 0.125, ((0, 128),)),
        "down_proj": scatter_about(key_of[6], (HELD, F, D), F ** -0.5, 0.25, ((0, 128),)),
        "query_in": scatter_about(key_of[7], (SEQUENCE_COUNT, WINDOW_LENGTH, KD), 1.0, 6.0, ((0, 16), (1, 8))),
        "key_in": draw_key_in(jax.random.fold_in(key_of[15], 71), 0),
        "value_in": scatter_about(key_of[9], (SEQUENCE_COUNT, WINDOW_LENGTH, VD), 1.0, 6.0, ((0, 16), (1, 8))),
        "gate_in": scatter_about(key_of[10], (SEQUENCE_COUNT, WINDOW_LENGTH, VD), 1.0, 6.0, ((0, 16), (1, 8))),
        "decay_logit": draw_decay_logit(jax.random.fold_in(key_of[15], 71), 0),
        "beta_logit": draw_beta_logit(jax.random.fold_in(key_of[15], 71), 0),
        "head_gain": jnp.clip(1.0 + 0.18 * jax.random.normal(key_of[13], (DK,), jnp.float32), 0.1, 1.9),
        "out_proj": scatter_about(key_of[14], (D, VD), VD ** -0.5, 0.125, ((1, 8),)),
    }


precise = lax.Precision.HIGHEST

def post_norm(hidden, gains):
    inverse_rms = lax.rsqrt(lax.optimization_barrier(jnp.mean(hidden * hidden, axis=-1, keepdims=True)) + 1e-06)
    return hidden * inverse_rms * gains

def block_step(memory, pieces):
    queries, key_rows, value_rows, strength, log_decay = pieces
    block_len = queries.shape[1]
    positions = jnp.arange(block_len)
    within = positions[:, None] >= positions[None, :]
    strict = positions[:, None] > positions[None, :]
    cumulative = jnp.cumsum(log_decay, axis=1)
    decay_mat = jnp.where(within, jnp.exp(jnp.where(within, cumulative[:, :, None] - cumulative[:, None, :], 0.0)), 0.0)
    inner_keys = jnp.einsum('htd,hsd->hts', key_rows, key_rows, precision=precise)
    lower_part = jnp.where(strict, strength[:, :, None] * decay_mat * inner_keys, 0.0)
    system = lower_part + jnp.eye(block_len, dtype=lower_part.dtype)
    recalled = jnp.einsum('hvd,htd->htv', memory, key_rows, precision=precise)
    rising = jnp.exp(cumulative)
    target = strength[:, :, None] * (value_rows - rising[:, :, None] * recalled)
    update = lax.linalg.triangular_solve(system, target, left_side=True, lower=True, unit_diagonal=True)
    scores = jnp.einsum('htd,hsd->hts', queries, key_rows, precision=precise) * decay_mat
    output = rising[:, :, None] * jnp.einsum('hvd,htd->htv', memory, queries, precision=precise)
    output = output + jnp.einsum('hts,hsv->htv', scores, update, precision=precise)
    last_log = cumulative[:, -1]
    fading = jnp.exp(last_log[:, None] - cumulative)
    memory = jnp.exp(last_log)[:, None, None] * memory + jnp.einsum('hsv,hsd->hvd', update * fading[:, :, None], key_rows, precision=precise)
    return (memory, output)

def gated_delta(query_rows, key_rows, value_rows, gate_rows, decay_rows, beta_rows, head_gain):
    length = query_rows.shape[0]
    head_dim = head_gain.shape[0]
    key_heads = query_rows.shape[1] // head_dim
    value_heads = value_rows.shape[1] // head_dim
    group_size = value_heads // key_heads

    def unit_rows(tensor):
        shaped = tensor.reshape(length, key_heads, head_dim)
        shaped = shaped * lax.rsqrt(lax.optimization_barrier(jnp.sum(shaped * shaped, axis=-1, keepdims=True)) + 1e-06)
        return jnp.repeat(shaped, group_size, axis=1)
    queries_unit = unit_rows(query_rows) * head_dim ** (-0.5)
    keys_unit = unit_rows(key_rows)
    values_all = value_rows.reshape(length, value_heads, head_dim)
    strength = jax.nn.sigmoid(beta_rows)
    log_decay = -jax.nn.softplus(decay_rows)
    block_count = length // BLOCK

    def to_blocks(tensor):
        moved_axes = jnp.moveaxis(tensor, 0, 1)
        shaped = moved_axes.reshape((value_heads, block_count, BLOCK) + tensor.shape[2:])
        return jnp.moveaxis(shaped, 1, 0)
    initial = jnp.zeros((value_heads, head_dim, head_dim), query_rows.dtype)
    final_memory, outputs = lax.scan(block_step, initial, (to_blocks(queries_unit), to_blocks(keys_unit), to_blocks(values_all), to_blocks(strength), to_blocks(log_decay)))
    output = jnp.moveaxis(outputs, 0, 1).reshape(value_heads, length, head_dim)
    output = jnp.moveaxis(output, 0, 1)
    gates_all = gate_rows.reshape(length, value_heads, head_dim)
    normed = output * lax.rsqrt(lax.optimization_barrier(jnp.mean(output * output, axis=-1, keepdims=True)) + 1e-06) * head_gain
    return (normed * jax.nn.silu(gates_all)).reshape(length, value_heads * head_dim)

def expert_backward(rows_in, rows_grad, gate_up, down_proj):
    hidden_units = down_proj.shape[0]
    contract_rows = (((1,), (1,)), ((), ()))
    contract_cols = (((0,), (0,)), ((), ()))
    projected = jnp.dot(rows_in.astype(jnp.float32), gate_up.astype(jnp.float32), preferred_element_type=jnp.float32)
    gate_part = projected[:, :hidden_units]
    up_part = projected[:, hidden_units:]
    sigma = jax.nn.sigmoid(gate_part)
    activated = gate_part * sigma
    product = (activated * up_part).astype(jnp.bfloat16)
    grad_act = lax.dot_general(rows_grad.astype(jnp.float32), down_proj.astype(jnp.float32), contract_rows, preferred_element_type=jnp.float32)
    grad_gate_part = grad_act * up_part * sigma * (1.0 + gate_part * (1.0 - sigma))
    grad_up_part = grad_act * activated
    grad_projected = jnp.concatenate([grad_gate_part, grad_up_part], axis=1).astype(jnp.bfloat16)
    rows_back = lax.dot_general(grad_projected.astype(jnp.float32), gate_up.astype(jnp.float32), contract_rows, preferred_element_type=jnp.float32).astype(jnp.bfloat16)
    weight_gate_up = lax.dot_general(rows_in.astype(jnp.float32), grad_projected.astype(jnp.float32), contract_cols, preferred_element_type=jnp.float32).astype(jnp.bfloat16)
    weight_down = lax.dot_general(product.astype(jnp.float32), rows_grad.astype(jnp.float32), contract_cols, preferred_element_type=jnp.float32).astype(jnp.bfloat16)
    return (rows_back, weight_gate_up, weight_down)

def reference(hidden_in, grad_out, post_gain, route_ids, route_weight, gate_up, down_proj, query_in, key_in, value_in, gate_in, decay_logit, beta_logit, head_gain, out_proj):
    flat_hidden = hidden_in.reshape(TOKENS, D).astype(jnp.float32)
    normed, norm_back = jax.vjp(lambda tensor: post_norm(tensor, post_gain), flat_hidden)
    moe_input = normed.astype(jnp.bfloat16)
    flat_grad = grad_out.reshape(TOKENS, D)
    slot_ids = route_ids.reshape(-1)
    slot_weights = route_weight.reshape(-1)
    input_ext = jnp.concatenate([moe_input, jnp.zeros((1, D), jnp.bfloat16)], axis=0)
    grad_ext = jnp.concatenate([flat_grad, jnp.zeros((1, D), jnp.bfloat16)], axis=0)
    weight_ext = jnp.concatenate([slot_weights, jnp.zeros((1,), jnp.float32)], axis=0)
    rows_most = HELD * EXPERT_ROW_LIMIT

    def per_expert(totals, expert):
        slots, = jnp.nonzero(slot_ids == expert, size=rows_most, fill_value=TOKENS * EXPERTS_PER_TOKEN)
        tokens_of = slots // EXPERTS_PER_TOKEN
        rows_in = input_ext[tokens_of]
        rows_grad = (grad_ext[tokens_of].astype(jnp.float32) * weight_ext[slots][:, None]).astype(jnp.bfloat16)
        rows_back, weight_gate_up, weight_down = expert_backward(rows_in, rows_grad, gate_up[expert], down_proj[expert])
        totals = totals.at[tokens_of].add(rows_back.astype(jnp.float32), mode='drop')
        return (totals, (weight_gate_up, weight_down))
    moe_grad, (grad_gate_up, grad_down) = lax.scan(per_expert, jnp.zeros((TOKENS, D), jnp.float32), jnp.arange(HELD, dtype=jnp.int32))
    norm_grad, = norm_back(moe_grad)
    grad_hidden = (flat_grad.astype(jnp.float32) + norm_grad).astype(jnp.bfloat16).reshape(SEQUENCE_COUNT, WINDOW_LENGTH, D)
    scale_factor = float(TOKENS) ** (-0.5)

    def per_sequence(totals, index):

        def forward(query_rows, key_rows, value_rows, gate_rows, decay_rows, beta_rows):
            return gated_delta(query_rows, key_rows, value_rows, gate_rows, decay_rows, beta_rows, head_gain)
        gated, core_back = jax.vjp(forward, query_in[index].astype(jnp.float32), key_in[index].astype(jnp.float32), value_in[index].astype(jnp.float32), gate_in[index].astype(jnp.float32), decay_logit[index].astype(jnp.float32), beta_logit[index].astype(jnp.float32))
        sequence_grad = grad_hidden[index]
        grad_gated = jnp.dot(sequence_grad.astype(jnp.float32), out_proj.astype(jnp.float32), preferred_element_type=jnp.float32)
        gradients = core_back(grad_gated)
        term = lax.dot_general(sequence_grad.astype(jnp.float32), gated.astype(jnp.bfloat16).astype(jnp.float32), (((0,), (0,)), ((), ())), preferred_element_type=jnp.float32)
        totals = totals + scale_factor * term
        return (totals, tuple((piece.astype(jnp.bfloat16) for piece in gradients)))
    grad_out_proj, gradients = lax.scan(per_sequence, jnp.zeros((D, VD), jnp.float32), jnp.arange(SEQUENCE_COUNT, dtype=jnp.int32))
    return (grad_hidden, gradients[0], gradients[1], gradients[2], gradients[3], gradients[4], gradients[5], grad_gate_up, grad_down, grad_out_proj)
```

```python
import functools

import jax
import jax.numpy as jnp
from jax import lax
from jax.experimental import pallas as pl
from jax.experimental.pallas import tpu as pltpu
from jax.sharding import PartitionSpec as P

F32 = jnp.float32
BF16 = jnp.bfloat16
EPS = 1e-6
MIB = 1 << 20

NN = (((1,), (0,)), ((), ()))
NT = (((1,), (1,)), ((), ()))
TN = (((0,), (0,)), ((), ()))


def dot(a, b, dims=NN):
    return lax.dot_general(a, b, dims, preferred_element_type=F32)


def halves(x):
    high = x.astype(BF16)
    return high, (x - high.astype(F32)).astype(BF16)


def dot_exact_left(a, b):
    high, low = halves(b)
    return dot(jnp.concatenate([a, a], axis=1), jnp.concatenate([high, low], axis=0))


def dot_split(a, b):
    ah, al = halves(a)
    bh, bl = halves(b)
    return dot(jnp.concatenate([ah, al, ah], axis=1), jnp.concatenate([bh, bh, bl], axis=0))


def dot_ones(a, ones):
    high = a.astype(BF16)
    rest = a - high.astype(F32)
    middle = rest.astype(BF16)
    low = (rest - middle.astype(F32)).astype(BF16)
    return dot(
        jnp.concatenate([high, middle, low], axis=1), jnp.concatenate([ones] * 3, axis=0)
    )


def iota(shape, axis):
    return lax.broadcasted_iota(jnp.int32, shape, axis)


def mask01(cond):
    return jnp.where(cond, 1.0, 0.0).astype(BF16)


def params(limit_mib=56, **kwargs):
    return pltpu.CompilerParams(vmem_limit_bytes=limit_mib * MIB, **kwargs)


def pack_kernel(q_ref, k_ref, v_ref, z_ref, decay_ref, beta_ref, out_ref):
    groups = out_ref.shape[0]
    heads = decay_ref.shape[1]
    row = iota((8 * groups, heads), 0)
    head = iota((8 * groups, heads), 1)
    kind = row % 8
    own = 2 * (row // 8) + kind % 2
    is_beta = (kind == 2) | (kind == 3)
    pick_decay = mask01((head == own) & ~is_beta)
    pick_beta = mask01((head == own) & is_beta)
    rows = dot(pick_decay, decay_ref[...], NT) + dot(pick_beta, beta_ref[...], NT)
    rows = rows.astype(BF16)
    for i in range(groups):
        out_ref[i, 0:128, 0:128] = q_ref[:, 128 * i : 128 * (i + 1)]
        out_ref[i, 0:128, 128:256] = k_ref[:, 128 * i : 128 * (i + 1)]
        out_ref[i, 0:128, 256:512] = v_ref[:, 256 * i : 256 * (i + 1)]
        out_ref[i, 0:128, 512:768] = z_ref[:, 256 * i : 256 * (i + 1)]
        out_ref[i, 128:136, 0:128] = rows[8 * i : 8 * (i + 1), :]
        out_ref[i, 128:136, 128:768] = jnp.zeros((8, 640), BF16)


def unpack_kernel(in_ref, q_ref, k_ref, v_ref, z_ref, decay_ref, beta_ref):
    groups = in_ref.shape[0]
    heads = decay_ref.shape[1]
    rows = []
    for i in range(groups):
        q_ref[:, 128 * i : 128 * (i + 1)] = in_ref[i, 0:128, 0:128]
        k_ref[:, 128 * i : 128 * (i + 1)] = in_ref[i, 0:128, 128:256]
        v_ref[:, 256 * i : 256 * (i + 1)] = in_ref[i, 0:128, 256:512]
        z_ref[:, 256 * i : 256 * (i + 1)] = in_ref[i, 0:128, 512:768]
        rows.append(in_ref[i, 128:136, 0:128].astype(F32))
    rows = jnp.concatenate(rows, axis=0).astype(BF16)
    row = iota((8 * groups, heads), 0)
    head = iota((8 * groups, heads), 1)
    kind = row % 8
    own = 2 * (row // 8) + kind % 2
    decay_ref[...] = dot(rows, mask01((head == own) & (kind < 2)), TN).astype(BF16)
    beta_ref[...] = dot(rows, mask01((head == own) & ((kind == 2) | (kind == 3))), TN).astype(BF16)


def slot_code(ids_ref, weight_ref):
    tokens, top = ids_ref.shape
    held = 128
    expert = iota((tokens, held), 1)
    named = jnp.zeros((tokens, held), F32)
    weight = jnp.zeros((tokens, held), F32)
    for k in range(top):
        hit = ids_ref[:, k : k + 1] == expert
        named = jnp.where(hit, 1.0, named)
        if weight_ref is not None:
            weight = jnp.where(hit, weight_ref[:, k : k + 1], weight)
    earlier = mask01(iota((tokens, tokens), 0) > iota((tokens, tokens), 1))
    rank = dot(earlier, named.astype(BF16))
    return jnp.where(named > 0.5, rank, -1.0), weight


def dispatch_kernel(hidden_ref, grad_ref, gain_ref, ids_ref, weight_ref, out_ref, both, pick, scale):
    rows = out_ref.shape[0]
    tokens, width = hidden_ref.shape
    cols = out_ref.shape[1]
    step = pl.program_id(0)

    @pl.when(step == 0)
    def _():
        hidden = hidden_ref[...].astype(F32)
        inverse = lax.rsqrt(jnp.mean(hidden * hidden, axis=-1, keepdims=True) + EPS)
        both[0:tokens, :] = (hidden * inverse * gain_ref[...]).astype(BF16)
        both[tokens:, :] = grad_ref[...]
        code, weight = slot_code(ids_ref, weight_ref)
        held = code.shape[1]
        spread = mask01(iota((rows, held), 0) // 8 == iota((rows, held), 1))
        wide = dot(spread, code.astype(BF16), NT)
        row = iota((rows, tokens), 0) % 8
        hit = wide == (row % 4).astype(F32)
        high = weight.astype(BF16)
        rest = weight - high.astype(F32)
        middle = rest.astype(BF16)
        low = (rest - middle.astype(F32)).astype(BF16)
        wide_weight = dot(spread, high, NT) + dot(spread, middle, NT) + dot(spread, low, NT)
        is_grad = row >= 4
        pick[:, 0:tokens] = mask01(hit & ~is_grad)
        pick[:, tokens:] = mask01(hit & is_grad)
        total = jnp.sum(jnp.where(hit, wide_weight, 0.0), axis=-1, keepdims=True)
        scale[...] = jnp.where(iota((rows, 1), 0) % 8 >= 4, total, 1.0)

    start = pl.multiple_of(step * cols, cols)
    chunk = dot(pick[...], both[:, pl.ds(start, cols)])
    out_ref[...] = (chunk * scale[...]).astype(BF16)


def expert_kernel(
    got_ref, up_hbm, down_hbm, back_ref, rows_ref, grads_ref, act_ref, gproj_ref,
    up_ref, down_ref, sems,
):
    hidden_units = down_ref.shape[0]
    width = down_ref.shape[1]
    copy_up = pltpu.make_async_copy(up_hbm, up_ref, sems.at[0])
    copy_down = pltpu.make_async_copy(down_hbm, down_ref, sems.at[1])
    copy_up.start()
    copy_down.start()
    count = rows_ref.shape[0]
    chunks = count // 64
    r = iota((128, 128), 0)
    c = iota((128, 128), 1)
    source = ((r % 64) // 4) * 8 + (r // 64) * 4 + r % 4
    gather = mask01(c == source)
    scatter = mask01(r == ((c % 64) // 4) * 8 + (c // 64) * 4 + c % 4)

    def separate(i, carry):
        block = got_ref[pl.ds(pl.multiple_of(i * 128, 128), 128), :]
        moved = dot(gather, block).astype(BF16)
        at = pl.multiple_of(i * 64, 64)
        rows_ref[pl.ds(at, 64), :] = moved[0:64]
        grads_ref[pl.ds(at, 64), :] = moved[64:128]
        return carry

    lax.fori_loop(0, chunks, separate, 0)
    copy_up.wait()
    copy_down.wait()

    def middle(j, carry):
        at = pl.multiple_of(j * 256, 256)
        gate = dot(rows_ref[...], up_ref[:, pl.ds(at, 256)])
        up = dot(rows_ref[...], up_ref[:, pl.ds(hidden_units + at, 256)])
        grad_act = dot(grads_ref[...], down_ref[pl.ds(at, 256), :], NT)
        sigma = jax.nn.sigmoid(gate)
        activated = gate * sigma
        act_ref[:, pl.ds(at, 256)] = (activated * up).astype(BF16)
        gproj_ref[:, pl.ds(at, 256)] = (
            grad_act * up * sigma * (1.0 + gate * (1.0 - sigma))
        ).astype(BF16)
        gproj_ref[:, pl.ds(hidden_units + at, 256)] = (grad_act * activated).astype(BF16)
        return carry

    lax.fori_loop(0, hidden_units // 256, middle, 0)

    def backward(j, carry):
        at = pl.multiple_of(j * 256, 256)
        left = dot(gproj_ref[...], up_ref[pl.ds(at, 256), :], NT).astype(BF16)
        right = dot(gproj_ref[...], up_ref[pl.ds(width // 2 + at, 256), :], NT).astype(BF16)
        for i in range(chunks):
            block = jnp.concatenate(
                [left[64 * i : 64 * (i + 1)], right[64 * i : 64 * (i + 1)]], axis=0
            )
            back_ref[128 * i : 128 * (i + 1), pl.ds(at, 256)] = dot(scatter, block).astype(BF16)
        return carry

    lax.fori_loop(0, width // 512, backward, 0)


def combine_kernel(
    back_ref, hidden_ref, grad_ref, gain_ref, ids_ref, proj_ref, hidden_grad_ref, out_ref
):
    tokens, width = hidden_ref.shape

    @pl.when(pl.program_id(0) == 0)
    def _():
        code, _ = slot_code(ids_ref, None)
        held = code.shape[1]
        rows = 8 * held
        spread = mask01(iota((held, rows), 0) == iota((held, rows), 1) // 8)
        wide = dot(code.astype(BF16), spread)
        place = iota((tokens, rows), 1) % 8
        hit = wide == (place % 4).astype(F32)
        first = mask01(hit & (place < 4))
        second = mask01(hit & (place >= 4))
        gain = gain_ref[...]
        hidden = hidden_ref[...].astype(F32)
        inverse = lax.rsqrt(jnp.mean(hidden * hidden, axis=-1, keepdims=True) + EPS)
        moe_grad = jnp.concatenate([dot(first, back_ref[...]), dot(second, back_ref[...])], axis=1)
        scaled = moe_grad * gain
        inner = jnp.mean(scaled * hidden, axis=-1, keepdims=True)
        norm_grad = inverse * scaled - hidden * (inverse * inverse * inverse * inner)
        hidden_grad_ref[...] = (grad_ref[...].astype(F32) + norm_grad).astype(BF16)

    out_ref[0] = dot(hidden_grad_ref[...], proj_ref[0]).astype(BF16)


def triangle(shape, strict=False):
    if strict:
        return iota(shape, 0) > iota(shape, 1)
    return iota(shape, 0) >= iota(shape, 1)


def vectors(att_ref, rows_scr, cols_scr):
    blocks = att_ref.shape[0]
    logits = jnp.concatenate(
        [att_ref[n, 128:136, 0:128].astype(F32) for n in range(blocks)], axis=0
    )
    kind = iota(logits.shape, 0) % 8
    upto = mask01(iota((128, 128), 0) <= iota((128, 128), 1))
    softplus = jnp.maximum(logits, 0.0) + jnp.log1p(jnp.exp(-jnp.abs(logits)))
    cumulative = dot_ones(-softplus, upto)
    strength = jax.nn.sigmoid(logits)
    fading = jnp.exp(cumulative[:, 127:128] - cumulative)
    rows = jnp.where(
        kind < 2,
        cumulative,
        jnp.where(kind < 4, strength, jnp.where(kind < 6, jnp.exp(cumulative), fading)),
    )
    cols = jnp.transpose(
        jnp.concatenate([rows, jnp.zeros((128 - rows.shape[0], 128), F32)], axis=0)
    )
    for n in range(blocks):
        rows_scr[n] = rows[8 * n : 8 * (n + 1)]
        cols_scr[n, :, 0:8] = cols[:, 8 * n : 8 * (n + 1)]
    return logits


def unit_scale(x, factor):
    xf = x.astype(F32)
    return lax.rsqrt(jnp.sum(xf * xf, axis=-1, keepdims=True) + EPS) * factor


def decay_matrix(col, row):
    within = triangle((128, 128))
    return jnp.where(within, jnp.exp(jnp.minimum(col - row, 0.0)), 0.0)


def forward_kernel(
    att_ref, gain_ref,
    gated_ref, tinv_ref, pair_ref, upd_ref, eks_ref, eqs_ref, mem_ref, core_ref,
    rows_scr, cols_scr, tri_scr, score_scr, state_scr,
):
    blocks = att_ref.shape[0]
    dim = 128
    vectors(att_ref, rows_scr, cols_scr)
    strict = triangle((dim, dim), strict=True)
    r = iota((dim, dim), 0)
    c = iota((dim, dim), 1)

    def inverse(n, carry):
        q = att_ref[n, 0:128, 0:128]
        k = att_ref[n, 0:128, 128:256]
        rows = rows_scr[n]
        cols = cols_scr[n]
        rk = unit_scale(k, 1.0)
        rq = unit_scale(q, dim**-0.5)
        rk_row = jnp.transpose(jnp.broadcast_to(rk, (dim, dim)))
        both = dot(jnp.concatenate([k, q], axis=0), k, NT)
        kk = both[0:128] * (rk * rk_row)
        qk = both[128:256] * (rq * rk_row)
        for h in range(2):
            decay = decay_matrix(cols[:, h : h + 1], rows[h : h + 1, :])
            low = jnp.where(strict, cols[:, 2 + h : 3 + h] * decay * kk, 0.0)
            inv = jnp.where(r == c, 1.0, 0.0) - jnp.where(r // 2 == c // 2, low, 0.0)
            size = 2
            while size < dim:
                level = (r // (2 * size) == c // (2 * size)) & (r // size != c // size)
                inv = inv - dot_split(dot_split(inv, jnp.where(level, low, 0.0)), inv)
                size *= 2
            tri_scr[n, :, 128 * h : 128 * (h + 1)] = inv
            score_scr[n, :, 128 * h : 128 * (h + 1)] = qk * decay
        return carry

    lax.fori_loop(0, blocks, inverse, 0)
    state_scr[...] = jnp.zeros_like(state_scr)
    gain = gain_ref[...]

    def advance(n, carry):
        q = att_ref[n, 0:128, 0:128]
        k = att_ref[n, 0:128, 128:256]
        cols = cols_scr[n]
        rows = rows_scr[n]
        rk = unit_scale(k, 1.0)
        rq = unit_scale(q, dim**-0.5)
        state = state_scr[...]
        mem_ref[n] = state.astype(BF16)
        recalled = dot_exact_left(jnp.concatenate([k, q], axis=0), state)
        kt = jnp.transpose(k)
        writes = []
        for h in range(2):
            at = slice(128 * h, 128 * (h + 1))
            beta = cols[:, 2 + h : 3 + h]
            rising = cols[:, 4 + h : 5 + h]
            fading = cols[:, 6 + h : 7 + h]
            eks = recalled[0:128, at] * (rk * rising)
            eqs = recalled[128:256, at] * (rq * rising)
            target = att_ref[n, 0:128, 256 + 128 * h : 384 + 128 * h].astype(F32) - eks
            inv = tri_scr[n, :, at]
            score = score_scr[n, :, at]
            update = dot_split(inv, beta * target)
            core = eqs + dot_split(score, update)
            writes.append((rk * fading) * update)
            z = att_ref[n, 0:128, 512 + 128 * h : 640 + 128 * h].astype(F32)
            normed = core * lax.rsqrt(jnp.mean(core * core, axis=-1, keepdims=True) + EPS) * gain
            gated_ref[n, :, at] = (normed * (z * jax.nn.sigmoid(z))).astype(BF16)
            inv_high, inv_low = halves(inv)
            tinv_ref[n, :, at] = inv_high
            tinv_ref[n, :, 256 + 128 * h : 384 + 128 * h] = inv_low
            pair_ref[n, :, at] = score.astype(BF16)
            upd_ref[n, :, at] = update.astype(BF16)
            eks_ref[n, :, at] = eks.astype(BF16)
            eqs_ref[n, :, at] = eqs.astype(BF16)
            core_ref[n, :, at] = core.astype(BF16)
        added = dot_exact_left(kt, jnp.concatenate(writes, axis=1))
        ends = jnp.concatenate(
            [jnp.broadcast_to(rows[4 + h : 5 + h, 127:128], (1, dim)) for h in range(2)], axis=1
        )
        state_scr[...] = ends * state + added
        return carry

    lax.fori_loop(0, blocks, advance, 0)


def backward_kernel(
    att_ref, dgated_ref, gain_ref, tinv_ref, pair_ref, upd_ref, eks_ref, eqs_ref, mem_ref, core_ref,
    out_ref,
    rows_scr, cols_scr, dcore_scr, push_scr, dq_state_scr, dtarget_scr, kds_scr, dmem_scr,
    state_scr, colbuf, rowbuf,
):
    blocks = att_ref.shape[0]
    dim = 128
    logits = vectors(att_ref, rows_scr, cols_scr)
    gain = gain_ref[...]
    within = triangle((dim, dim))
    strict = triangle((dim, dim), strict=True)

    def local(n, carry):
        q = att_ref[n, 0:128, 0:128]
        cols = cols_scr[n]
        rq = unit_scale(q, dim**-0.5)
        pushed = []
        for h in range(2):
            at = slice(128 * h, 128 * (h + 1))
            rising = cols[:, 4 + h : 5 + h]
            core = core_ref[n, :, at].astype(F32)
            z = att_ref[n, 0:128, 512 + 128 * h : 640 + 128 * h].astype(F32)
            grad = dgated_ref[n, :, at].astype(F32)
            sigma = jax.nn.sigmoid(z)
            inverse_rms = lax.rsqrt(jnp.mean(core * core, axis=-1, keepdims=True) + EPS)
            normed = core * inverse_rms
            out_ref[n, 0:128, 512 + 128 * h : 640 + 128 * h] = (
                grad * normed * gain * (sigma * (1.0 + z * (1.0 - sigma)))
            ).astype(BF16)
            dnormed = grad * gain * (z * sigma)
            dcore = inverse_rms * (
                dnormed - normed * jnp.mean(dnormed * normed, axis=-1, keepdims=True)
            )
            dcore_scr[n, :, at] = dcore
            push_scr[n, :, at] = dot(pair_ref[n, :, at], dcore.astype(BF16), TN)
            pushed.append((rq * rising) * dcore)
        dq_state_scr[n] = dot(q, jnp.concatenate(pushed, axis=1).astype(BF16), TN)
        return carry

    lax.fori_loop(0, blocks, local, 0)
    state_scr[...] = jnp.zeros_like(state_scr)

    def retreat(i, carry):
        n = blocks - 1 - i
        k = att_ref[n, 0:128, 128:256]
        cols = cols_scr[n]
        rows = rows_scr[n]
        rk = unit_scale(k, 1.0)
        state = state_scr[...]
        dmem_scr[n] = state
        read = dot_exact_left(k, state)
        erased = []
        for h in range(2):
            at = slice(128 * h, 128 * (h + 1))
            beta = cols[:, 2 + h : 3 + h]
            rising = cols[:, 4 + h : 5 + h]
            fading = cols[:, 6 + h : 7 + h]
            kds = read[:, at] * (rk * fading)
            kds_scr[n, :, at] = kds
            high, low = halves(push_scr[n, :, at] + kds)
            inv_high = tinv_ref[n, :, at]
            inv_low = tinv_ref[n, :, 256 + 128 * h : 384 + 128 * h]
            dtarget = dot(
                jnp.concatenate([inv_high, inv_low, inv_high], axis=0),
                jnp.concatenate([high, high, low], axis=0),
                TN,
            )
            dtarget_scr[n, :, at] = dtarget
            erased.append((rk * beta * rising) * dtarget)
        kt = jnp.transpose(k)
        ends = jnp.concatenate(
            [jnp.broadcast_to(rows[4 + h : 5 + h, 127:128], (1, dim)) for h in range(2)], axis=1
        )
        state_scr[...] = (
            ends * state + dq_state_scr[n] - dot_exact_left(kt, jnp.concatenate(erased, axis=1))
        )
        return carry

    lax.fori_loop(0, blocks, retreat, 0)
    last = iota((dim, 1), 0) == dim - 1

    def finish(n, carry):
        q = att_ref[n, 0:128, 0:128]
        k = att_ref[n, 0:128, 128:256]
        cols = cols_scr[n]
        rows = rows_scr[n]
        rk = unit_scale(k, 1.0)
        rq = unit_scale(q, dim**-0.5)
        rk_row = jnp.transpose(jnp.broadcast_to(rk, (dim, dim)))
        both = dot(jnp.concatenate([k, q], axis=0), k, NT)
        kk = both[0:128] * (rk * rk_row)
        qk = both[128:256] * (rq * rk_row)
        dqk = jnp.zeros((dim, dim), F32)
        dkk = jnp.zeros((dim, dim), F32)
        read_out = []
        erase = []
        write = []
        for h in range(2):
            at = slice(128 * h, 128 * (h + 1))
            beta = cols[:, 2 + h : 3 + h]
            rising = cols[:, 4 + h : 5 + h]
            fading = cols[:, 6 + h : 7 + h]
            decay = decay_matrix(cols[:, h : h + 1], rows[h : h + 1, :])
            update = upd_ref[n, :, at]
            dcore = dcore_scr[n, :, at]
            dtarget = dtarget_scr[n, :, at]
            kds = kds_scr[n, :, at]
            outer = dot(
                jnp.concatenate([dcore.astype(BF16), dtarget.astype(BF16)], axis=0), update, NT
            )
            dscore = jnp.where(within, outer[0:128], 0.0) * decay
            dlow = jnp.where(strict, -outer[128:256], 0.0) * decay
            dqk = dqk + dscore
            dkk = dkk + dlow * beta
            dlow_kk = dlow * kk
            eks = eks_ref[n, :, at].astype(F32)
            eqs = eqs_ref[n, :, at].astype(F32)
            value = att_ref[n, 0:128, 256 + 128 * h : 384 + 128 * h].astype(F32)
            out_ref[n, 0:128, 256 + 128 * h : 384 + 128 * h] = (beta * dtarget).astype(BF16)
            dbeta = jnp.sum(dtarget * (value - eks) + dlow_kk, axis=-1, keepdims=True)
            flow = dscore * qk + dlow_kk * beta
            kept = update.astype(F32) * kds
            from_write = jnp.sum(kept, axis=-1, keepdims=True)
            through = jnp.sum(
                mem_ref[n, :, at].astype(F32) * dmem_scr[n, :, at], keepdims=True
            ) * rows[4 + h : 5 + h, 127:128]
            dlog = (
                jnp.sum(flow + dcore * eqs - (beta * dtarget) * eks, axis=-1, keepdims=True)
                - from_write
            )
            dlog = dlog + jnp.where(last, jnp.sum(from_write, keepdims=True) + through, 0.0)
            colbuf[n, :, h : h + 1] = dlog
            colbuf[n, :, 2 + h : 3 + h] = dbeta
            rowbuf[n, h : h + 1, :] = -jnp.sum(flow, axis=0, keepdims=True)
            read_out.append(rising * dcore)
            erase.append((-(beta * rising)) * dtarget)
            write.append(fading * update.astype(F32))
        mem = mem_ref[n]
        top = jnp.concatenate(
            [jnp.concatenate(read_out, axis=1), jnp.concatenate(erase, axis=1)], axis=0
        ).astype(BF16)
        from_mem = dot(top, mem, NT)
        dk = from_mem[128:256] + dot(
            jnp.concatenate(write, axis=1).astype(BF16), dmem_scr[n].astype(BF16), NT
        )
        dq = from_mem[0:128] + dot((dqk * rk_row).astype(BF16), k)
        dk = dk + dot((dqk * rq).astype(BF16), q, TN)
        dk = dk + dot(((dkk + jnp.transpose(dkk)) * rk_row).astype(BF16), k)
        qf = q.astype(F32)
        kf = k.astype(F32)
        dq = rq * (dq - qf * ((rq * rq * dim) * jnp.sum(qf * dq, axis=-1, keepdims=True)))
        dk = rk * (dk - kf * ((rk * rk) * jnp.sum(kf * dk, axis=-1, keepdims=True)))
        out_ref[n, 0:128, 0:128] = dq.astype(BF16)
        out_ref[n, 0:128, 128:256] = dk.astype(BF16)
        return carry

    colbuf[...] = jnp.zeros_like(colbuf)
    rowbuf[...] = jnp.zeros_like(rowbuf)
    lax.fori_loop(0, blocks, finish, 0)
    cols = jnp.concatenate(
        [colbuf[n, :, 0:8] for n in range(blocks)]
        + [jnp.zeros((dim, dim - 8 * blocks), F32)],
        axis=1,
    )
    grads = jnp.transpose(cols)[0 : 8 * blocks] + jnp.concatenate(
        [rowbuf[n] for n in range(blocks)], axis=0
    )
    kind = iota(grads.shape, 0) % 8
    after = mask01(iota((dim, dim), 0) >= iota((dim, dim), 1))
    sigma = jax.nn.sigmoid(logits)
    grads = jnp.where(
        kind < 2, -dot_ones(grads, after) * sigma, grads * sigma * (1.0 - sigma)
    ).astype(BF16)
    for n in range(blocks):
        out_ref[n, 128:136, 0:128] = grads[8 * n : 8 * (n + 1)]
        out_ref[n, 128:136, 128:768] = jnp.zeros((8, 640), BF16)


def sum_kernel(in_ref, out_ref):
    out_ref[...] = jnp.sum(in_ref[...].astype(F32), axis=0)


def shape(dims, dtype=BF16):
    return jax.ShapeDtypeStruct(dims, dtype)


def vmem_call(kernel, outs, scratch=(), flops=0, moved=0, limit=56):
    return pl.pallas_call(
        kernel,
        out_shape=outs,
        scratch_shapes=list(scratch),
        compiler_params=params(limit),
        cost_estimate=pl.CostEstimate(flops=flops, bytes_accessed=moved, transcendentals=0),
    )


def run_forward(att, gain):
    blocks = att.shape[0]
    square = (blocks, 128, 256)
    return vmem_call(
        forward_kernel,
        [shape(square), shape((blocks, 128, 512))] + [shape(square)] * 6,
        [
            pltpu.VMEM((blocks, 8, 128), F32),
            pltpu.VMEM((blocks, 128, 128), F32),
            pltpu.VMEM(square, F32),
            pltpu.VMEM(square, F32),
            pltpu.VMEM((128, 256), F32),
        ],
        flops=12 * 10**9,
        moved=8 * MIB,
    )(att, gain)


def run_backward(att, dgated, gain, saved):
    blocks = att.shape[0]
    square = (blocks, 128, 256)
    return vmem_call(
        backward_kernel,
        shape((blocks, 136, 768)),
        [pltpu.VMEM((blocks, 8, 128), F32), pltpu.VMEM((blocks, 128, 128), F32)]
        + [pltpu.VMEM(square, F32)] * 6
        + [
            pltpu.VMEM((128, 256), F32),
            pltpu.VMEM((blocks, 128, 128), F32),
            pltpu.VMEM((blocks, 8, 128), F32),
        ],
        flops=12 * 10**9,
        moved=8 * MIB,
    )(att, dgated, gain, *saved)


def body(
    hidden_in, grad_out, post_gain, route_ids, route_weight, gate_up, down_proj,
    query_in, key_in, value_in, gate_in, decay_logit, beta_logit, head_gain, out_proj,
):
    ctx = lax.axis_size("ctx")
    exp = lax.axis_size("exp")
    devices = ctx * exp
    tokens, width = hidden_in.shape[1:]
    hidden_units = down_proj.shape[1]
    slots = 4 * devices
    hidden = hidden_in[0]
    grad = grad_out[0]
    gain = post_gain.reshape(1, width)
    ids = route_ids[0]

    steps = 4
    whole = lambda *dims: pl.BlockSpec(dims, lambda i: (0,) * len(dims))
    rows = pl.pallas_call(
        dispatch_kernel,
        grid=(steps,),
        in_specs=[
            whole(tokens, width), whole(tokens, width), whole(1, width),
            whole(*ids.shape), whole(*ids.shape),
        ],
        out_specs=pl.BlockSpec((2 * slots, width // steps), lambda i: (0, i)),
        out_shape=shape((2 * slots, width)),
        scratch_shapes=[
            pltpu.VMEM((2 * tokens, width), BF16),
            pltpu.VMEM((2 * slots, 2 * tokens), BF16),
            pltpu.VMEM((2 * slots, 1), F32),
        ],
        compiler_params=params(),
        cost_estimate=pl.CostEstimate(flops=10**9, bytes_accessed=6 * MIB, transcendentals=0),
    )(hidden, grad, gain, ids, route_weight[0])
    got = lax.all_to_all(
        rows.reshape(devices, 8, width), ("ctx", "exp"), split_axis=0, concat_axis=0, tiled=True
    ).reshape(2 * slots, width)

    packed = vmem_call(pack_kernel, shape((ctx, 136, 768)), moved=4 * MIB)(
        query_in[0], key_in[0], value_in[0], gate_in[0], decay_logit[0], beta_logit[0]
    )
    att = lax.all_to_all(packed, "ctx", split_axis=0, concat_axis=0, tiled=True)
    proj_all = lax.all_gather(out_proj, "ctx", axis=0, tiled=False)

    gain_heads = head_gain.reshape(1, 128)
    gated, *saved = run_forward(att, gain_heads)

    got, gated, saved = lax.optimization_barrier((got, gated, saved))
    back, rows_in, rows_grad, act, gproj = pl.pallas_call(
        expert_kernel,
        in_specs=[
            pl.BlockSpec(memory_space=pltpu.VMEM),
            pl.BlockSpec(memory_space=pl.ANY),
            pl.BlockSpec(memory_space=pl.ANY),
        ],
        out_shape=[
            shape((2 * slots, width // 2)), shape((slots, width)), shape((slots, width)),
            shape((slots, hidden_units)), shape((slots, 2 * hidden_units)),
        ],
        scratch_shapes=[
            pltpu.VMEM((width, 2 * hidden_units), BF16),
            pltpu.VMEM((hidden_units, width), BF16),
            pltpu.SemaphoreType.DMA((2,)),
        ],
        compiler_params=params(),
        cost_estimate=pl.CostEstimate(
            flops=6 * 10**9, bytes_accessed=18 * MIB, transcendentals=0
        ),
    )(got, gate_up[0], down_proj[0])
    returned = lax.all_to_all(
        back.reshape(devices, 8, width // 2), ("ctx", "exp"), split_axis=0, concat_axis=0, tiled=True
    ).reshape(2 * slots, width // 2)
    grad_gate_up = dot(rows_in, gproj, TN).astype(BF16)
    grad_down = dot(act, rows_grad, TN).astype(BF16)
    returned, grad_gate_up, grad_down = lax.optimization_barrier(
        (returned, grad_gate_up, grad_down)
    )

    grad_hidden, dgated = pl.pallas_call(
        combine_kernel,
        grid=(ctx,),
        in_specs=[
            whole(2 * slots, width // 2), whole(tokens, width), whole(tokens, width),
            whole(1, width), whole(*ids.shape),
            pl.BlockSpec((1, width, 256), lambda i: (i, 0, 0)),
        ],
        out_specs=[whole(tokens, width), pl.BlockSpec((1, tokens, 256), lambda i: (i, 0, 0))],
        out_shape=[shape((tokens, width)), shape((ctx, tokens, 256))],
        compiler_params=params(),
        cost_estimate=pl.CostEstimate(flops=2 * 10**9, bytes_accessed=13 * MIB, transcendentals=0),
    )(returned, hidden, grad, gain, ids, proj_all)
    dgated = lax.all_to_all(dgated, "ctx", split_axis=0, concat_axis=0, tiled=True)
    hidden_all = lax.all_gather(grad_hidden, "ctx", axis=0, tiled=True)

    grads = run_backward(att, dgated, gain_heads, saved)
    grads = lax.all_to_all(grads, "ctx", split_axis=0, concat_axis=0, tiled=True)

    scale = float(tokens * devices) ** (-0.5)
    term = (scale * dot(hidden_all, gated.reshape(-1, 256), TN)).astype(BF16)
    terms = lax.all_to_all(
        term.reshape(exp, width // exp, 256), "exp", split_axis=0, concat_axis=0, tiled=True
    )
    grad_out_proj = vmem_call(sum_kernel, shape((width // exp, 256), F32), moved=MIB)(terms)

    dq, dk, dv, dz, ddecay, dbeta = vmem_call(
        unpack_kernel,
        [
            shape(query_in.shape[1:]), shape(key_in.shape[1:]), shape(value_in.shape[1:]),
            shape(gate_in.shape[1:]), shape(decay_logit.shape[1:]), shape(beta_logit.shape[1:]),
        ],
        moved=4 * MIB,
    )(grads)
    return (
        grad_hidden[None], dq[None], dk[None], dv[None], dz[None], ddecay[None], dbeta[None],
        grad_gate_up[None], grad_down[None], grad_out_proj,
    )


def solution(mesh):
    tokens = P("exp", "ctx", None)
    experts = P(("ctx", "exp"), None, None)
    return jax.shard_map(
        body,
        mesh=mesh,
        in_specs=(
            tokens, tokens, P(), tokens, tokens, experts, experts,
            tokens, tokens, tokens, tokens, tokens, tokens, P(), P(None, "ctx"),
        ),
        out_specs=(
            tokens, tokens, tokens, tokens, tokens, tokens, tokens,
            experts, experts, P("exp", "ctx"),
        ),
        check_vma=False,
    )
```

```python
import functools

import jax
import jax.numpy as jnp
from jax import lax
from jax.experimental import pallas as pl
from jax.experimental.pallas import tpu as pltpu
from jax.sharding import PartitionSpec as P

F32 = jnp.float32
BF16 = jnp.bfloat16
EPS = 1e-6
MIB = 1 << 20
INVERSE_GROUP = 4

NN = (((1,), (0,)), ((), ()))
NT = (((1,), (1,)), ((), ()))
TN = (((0,), (0,)), ((), ()))


def dot(a, b, dims=NN):
    return lax.dot_general(a, b, dims, preferred_element_type=F32)


def halves(x):
    high = x.astype(BF16)
    return high, (x - high.astype(F32)).astype(BF16)


def dot_exact_left(a, b):
    high, low = halves(b)
    return dot(jnp.concatenate([a, a], axis=1), jnp.concatenate([high, low], axis=0))


def dot_split(a, b):
    ah, al = halves(a)
    bh, bl = halves(b)
    return dot(jnp.concatenate([ah, al, ah], axis=1), jnp.concatenate([bh, bh, bl], axis=0))


def dot_ones(a, ones):
    high = a.astype(BF16)
    rest = a - high.astype(F32)
    middle = rest.astype(BF16)
    low = (rest - middle.astype(F32)).astype(BF16)
    return dot(
        jnp.concatenate([high, middle, low], axis=1), jnp.concatenate([ones] * 3, axis=0)
    )


def iota(shape, axis):
    return lax.broadcasted_iota(jnp.int32, shape, axis)


def mask01(cond):
    return jnp.where(cond, 1.0, 0.0).astype(BF16)


def params(limit_mib=56, **kwargs):
    return pltpu.CompilerParams(vmem_limit_bytes=limit_mib * MIB, **kwargs)


def pack_kernel(q_ref, k_ref, v_ref, z_ref, decay_ref, beta_ref, out_ref):
    groups = out_ref.shape[0]
    heads = decay_ref.shape[0]
    row = iota((8 * groups, heads), 0)
    head = iota((8 * groups, heads), 1)
    kind = row % 8
    own = 2 * (row // 8) + kind % 2
    is_beta = (kind == 2) | (kind == 3)
    pick_decay = mask01((head == own) & ~is_beta)
    pick_beta = mask01((head == own) & is_beta)
    rows = dot(pick_decay, decay_ref[...]) + dot(pick_beta, beta_ref[...])
    rows = rows.astype(BF16)
    for i in range(groups):
        out_ref[i, 0:128, 0:128] = q_ref[:, 128 * i : 128 * (i + 1)]
        out_ref[i, 0:128, 128:256] = k_ref[:, 128 * i : 128 * (i + 1)]
        out_ref[i, 0:128, 256:512] = v_ref[:, 256 * i : 256 * (i + 1)]
        out_ref[i, 0:128, 512:768] = z_ref[:, 256 * i : 256 * (i + 1)]
        out_ref[i, 128:136, 0:128] = rows[8 * i : 8 * (i + 1), :]
        out_ref[i, 128:136, 128:768] = jnp.zeros((8, 640), BF16)


def unpack_kernel(in_ref, q_ref, k_ref, v_ref, z_ref, decay_ref, beta_ref):
    groups = in_ref.shape[0]
    heads = decay_ref.shape[0]
    rows = []
    for i in range(groups):
        q_ref[:, 128 * i : 128 * (i + 1)] = in_ref[i, 0:128, 0:128]
        k_ref[:, 128 * i : 128 * (i + 1)] = in_ref[i, 0:128, 128:256]
        v_ref[:, 256 * i : 256 * (i + 1)] = in_ref[i, 0:128, 256:512]
        z_ref[:, 256 * i : 256 * (i + 1)] = in_ref[i, 0:128, 512:768]
        rows.append(in_ref[i, 128:136, 0:128].astype(F32))
    rows = jnp.concatenate(rows, axis=0).astype(BF16)
    row = iota((heads, 8 * groups), 1)
    head = iota((heads, 8 * groups), 0)
    kind = row % 8
    own = 2 * (row // 8) + kind % 2
    decay_ref[...] = dot(mask01((head == own) & (kind < 2)), rows).astype(BF16)
    beta_ref[...] = dot(mask01((head == own) & ((kind == 2) | (kind == 3))), rows).astype(BF16)


def slot_code(ids_ref, weight_ref):
    top, _, tokens = ids_ref.shape
    held = 128
    expert = iota((held, tokens), 0)
    named = jnp.zeros((held, tokens), F32)
    weight = jnp.zeros((held, tokens), F32)
    for k in range(top):
        hit = ids_ref[k] == expert
        named = jnp.where(hit, 1.0, named)
        if weight_ref is not None:
            weight = jnp.where(hit, weight_ref[k], weight)
    earlier = mask01(iota((tokens, tokens), 0) < iota((tokens, tokens), 1))
    rank = dot(named.astype(BF16), earlier)
    return jnp.where(named > 0.5, rank, -1.0), weight


def dispatch_kernel(hidden_ref, grad_ref, gain_ref, ids_ref, weight_ref, out_ref, both, pick, scale):
    rows = out_ref.shape[0]
    tokens, width = hidden_ref.shape
    cols = out_ref.shape[1]
    step = pl.program_id(0)

    @pl.when(step == 0)
    def _():
        hidden = hidden_ref[...].astype(F32)
        inverse = lax.rsqrt(jnp.mean(hidden * hidden, axis=-1, keepdims=True) + EPS)
        both[0:tokens, :] = (hidden * inverse * gain_ref[...]).astype(BF16)
        both[tokens:, :] = grad_ref[...]
        code, weight = slot_code(ids_ref, weight_ref)
        held = code.shape[0]
        spread = mask01(iota((rows, held), 0) // 8 == iota((rows, held), 1))
        wide = dot(spread, code.astype(BF16))
        row = iota((rows, tokens), 0) % 8
        hit = wide == (row % 4).astype(F32)
        high = weight.astype(BF16)
        rest = weight - high.astype(F32)
        middle = rest.astype(BF16)
        low = (rest - middle.astype(F32)).astype(BF16)
        wide_weight = dot(spread, high) + dot(spread, middle) + dot(spread, low)
        is_grad = row >= 4
        pick[:, 0:tokens] = mask01(hit & ~is_grad)
        pick[:, tokens:] = mask01(hit & is_grad)
        total = jnp.sum(jnp.where(hit, wide_weight, 0.0), axis=-1, keepdims=True)
        scale[...] = jnp.where(iota((rows, 1), 0) % 8 >= 4, total, 1.0)

    start = pl.multiple_of(step * cols, cols)
    chunk = dot(pick[...], both[:, pl.ds(start, cols)])
    out_ref[...] = (chunk * scale[...]).astype(BF16)


def expert_kernel(
    got_ref, up_hbm, down_hbm, back_ref, rows_ref, grads_ref, act_ref, gproj_ref,
    up_ref, down_ref, sems,
):
    hidden_units = down_ref.shape[0]
    width = down_ref.shape[1]
    copy_up = pltpu.make_async_copy(up_hbm, up_ref, sems.at[0])
    copy_down = pltpu.make_async_copy(down_hbm, down_ref, sems.at[1])
    copy_up.start()
    copy_down.start()
    count = rows_ref.shape[0]
    chunks = count // 64
    r = iota((128, 128), 0)
    c = iota((128, 128), 1)
    source = ((r % 64) // 4) * 8 + (r // 64) * 4 + r % 4
    gather = mask01(c == source)
    scatter = mask01(r == ((c % 64) // 4) * 8 + (c // 64) * 4 + c % 4)

    def separate(i, carry):
        block = got_ref[pl.ds(pl.multiple_of(i * 128, 128), 128), :]
        moved = dot(gather, block).astype(BF16)
        at = pl.multiple_of(i * 64, 64)
        rows_ref[pl.ds(at, 64), :] = moved[0:64]
        grads_ref[pl.ds(at, 64), :] = moved[64:128]
        return carry

    lax.fori_loop(0, chunks, separate, 0)
    copy_up.wait()
    copy_down.wait()

    def middle(j, carry):
        at = pl.multiple_of(j * 256, 256)
        gate = dot(rows_ref[...], up_ref[:, pl.ds(at, 256)])
        up = dot(rows_ref[...], up_ref[:, pl.ds(hidden_units + at, 256)])
        grad_act = dot(grads_ref[...], down_ref[pl.ds(at, 256), :], NT)
        sigma = jax.nn.sigmoid(gate)
        activated = gate * sigma
        act_ref[:, pl.ds(at, 256)] = (activated * up).astype(BF16)
        gproj_ref[:, pl.ds(at, 256)] = (
            grad_act * up * sigma * (1.0 + gate * (1.0 - sigma))
        ).astype(BF16)
        gproj_ref[:, pl.ds(hidden_units + at, 256)] = (grad_act * activated).astype(BF16)
        return carry

    lax.fori_loop(0, hidden_units // 256, middle, 0)

    def backward(j, carry):
        at = pl.multiple_of(j * 256, 256)
        left = dot(gproj_ref[...], up_ref[pl.ds(at, 256), :], NT).astype(BF16)
        right = dot(gproj_ref[...], up_ref[pl.ds(width // 2 + at, 256), :], NT).astype(BF16)
        for i in range(chunks):
            block = jnp.concatenate(
                [left[64 * i : 64 * (i + 1)], right[64 * i : 64 * (i + 1)]], axis=0
            )
            back_ref[128 * i : 128 * (i + 1), pl.ds(at, 256)] = dot(scatter, block).astype(BF16)
        return carry

    lax.fori_loop(0, width // 512, backward, 0)


def combine_kernel(back_ref, hidden_ref, grad_ref, gain_ref, ids_ref, out_ref):
    tokens, width = hidden_ref.shape
    code, _ = slot_code(ids_ref, None)
    held = code.shape[0]
    code = jnp.transpose(code)
    rows = 8 * held
    spread = mask01(iota((held, rows), 0) == iota((held, rows), 1) // 8)
    wide = dot(code.astype(BF16), spread)
    place = iota((tokens, rows), 1) % 8
    hit = wide == (place % 4).astype(F32)
    first = mask01(hit & (place < 4))
    second = mask01(hit & (place >= 4))
    hidden = hidden_ref[...].astype(F32)
    inverse = lax.rsqrt(jnp.mean(hidden * hidden, axis=-1, keepdims=True) + EPS)
    moe_grad = jnp.concatenate([dot(first, back_ref[...]), dot(second, back_ref[...])], axis=1)
    scaled = moe_grad * gain_ref[...]
    inner = jnp.mean(scaled * hidden, axis=-1, keepdims=True)
    norm_grad = inverse * scaled - hidden * (inverse * inverse * inverse * inner)
    out_ref[...] = (grad_ref[...].astype(F32) + norm_grad).astype(BF16)


def project_first_kernel(a_ref, b_ref, c_ref, d_ref, proj_ref, gated_ref, grad_ref, term_ref):
    project((a_ref, b_ref, c_ref, d_ref), proj_ref, gated_ref, 0, grad_ref, None, term_ref, 1.0)


def project_last_kernel(
    a_ref, b_ref, c0_ref, c1_ref, d0_ref, d1_ref, proj_ref, gated_ref, sofar_ref,
    grad_ref, term_ref, *, scale
):
    pieces = (a_ref, b_ref, c0_ref, c1_ref, d0_ref, d1_ref)
    project(pieces, proj_ref, gated_ref, 4, grad_ref, sofar_ref, term_ref, scale)


def project(pieces, proj_ref, gated_ref, slot, grad_ref, sofar_ref, term_ref, scale):
    row = 0
    for pair in (pieces[:2], pieces[2:]):
        block = jnp.concatenate([piece[...] for piece in pair], axis=0)
        out = dot(block, proj_ref[...])
        for i in range(2):
            grad_ref[row + i] = out[128 * i : 128 * (i + 1)]
        row += 2
    left = jnp.concatenate([gated_ref[slot + i] for i in range(4)], axis=1)
    for j in range(term_ref.shape[0] // 2):
        at = slice(256 * j, 256 * (j + 1))
        right = jnp.concatenate([piece[:, at] for piece in pieces], axis=0)
        term = dot(left, right)
        for i in range(2):
            part = term[:, 128 * i : 128 * (i + 1)]
            if sofar_ref is not None:
                part = part + sofar_ref[2 * j + i]
            term_ref[2 * j + i] = (part * scale).astype(term_ref.dtype)


def triangle(shape, strict=False):
    if strict:
        return iota(shape, 0) > iota(shape, 1)
    return iota(shape, 0) >= iota(shape, 1)


def vectors(att_ref, rows_scr, cols_scr):
    blocks = att_ref.shape[0]
    logits = jnp.concatenate(
        [att_ref[n, 128:136, 0:128].astype(F32) for n in range(blocks)], axis=0
    )
    kind = iota(logits.shape, 0) % 8
    upto = mask01(iota((128, 128), 0) <= iota((128, 128), 1))
    softplus = jnp.maximum(logits, 0.0) + jnp.log1p(jnp.exp(-jnp.abs(logits)))
    cumulative = dot_ones(-softplus, upto)
    strength = jax.nn.sigmoid(logits)
    fading = jnp.exp(cumulative[:, 127:128] - cumulative)
    rows = jnp.where(
        kind < 2,
        cumulative,
        jnp.where(kind < 4, strength, jnp.where(kind < 6, jnp.exp(cumulative), fading)),
    )
    cols = jnp.transpose(
        jnp.concatenate([rows, jnp.zeros((128 - rows.shape[0], 128), F32)], axis=0)
    )
    for n in range(blocks):
        rows_scr[n] = rows[8 * n : 8 * (n + 1)]
        cols_scr[n, :, 0:8] = cols[:, 8 * n : 8 * (n + 1)]
    return logits


def unit_scale(x, factor):
    xf = x.astype(F32)
    return lax.rsqrt(jnp.sum(xf * xf, axis=-1, keepdims=True) + EPS) * factor


def decay_matrix(col, row):
    within = triangle((128, 128))
    return jnp.where(within, jnp.exp(jnp.minimum(col - row, 0.0)), 0.0)


def forward_kernel(
    slot_ref, att_ref, gain_ref,
    gated_ref, tinv_ref, pair_ref, upd_ref, eks_ref, eqs_ref, mem_ref, core_ref,
    rows_scr, cols_scr, tri_scr, score_scr, state_scr,
):
    blocks = att_ref.shape[0]
    dim = 128
    vectors(att_ref, rows_scr, cols_scr)
    strict = triangle((dim, dim), strict=True)
    r = iota((dim, dim), 0)
    c = iota((dim, dim), 1)

    def inverse(i, carry):
        lows = []
        scores = []
        group = [INVERSE_GROUP * i + g for g in range(INVERSE_GROUP)]
        for n in group:
            q = att_ref[n, 0:128, 0:128]
            k = att_ref[n, 0:128, 128:256]
            rows = rows_scr[n]
            cols = cols_scr[n]
            rk = unit_scale(k, 1.0)
            rq = unit_scale(q, dim**-0.5)
            rk_row = jnp.transpose(jnp.broadcast_to(rk, (dim, dim)))
            both = dot(jnp.concatenate([k, q], axis=0), k, NT)
            kk = both[0:128] * (rk * rk_row)
            qk = both[128:256] * (rq * rk_row)
            for h in range(2):
                decay = decay_matrix(cols[:, h : h + 1], rows[h : h + 1, :])
                lows.append(jnp.where(strict, cols[:, 2 + h : 3 + h] * decay * kk, 0.0))
                scores.append(qk * decay)
        invs = [
            jnp.where(r == c, 1.0, 0.0) - jnp.where(r // 2 == c // 2, low, 0.0) for low in lows
        ]
        size = 2
        while size < dim:
            level = (r // (2 * size) == c // (2 * size)) & (r // size != c // size)
            steps = [
                dot_split(inv, jnp.where(level, low, 0.0)) for inv, low in zip(invs, lows)
            ]
            invs = [inv - dot_split(step, inv) for inv, step in zip(invs, steps)]
            size *= 2
        for g, n in enumerate(group):
            for h in range(2):
                tri_scr[n, :, 128 * h : 128 * (h + 1)] = invs[2 * g + h]
                score_scr[n, :, 128 * h : 128 * (h + 1)] = scores[2 * g + h]
        return carry

    lax.fori_loop(0, blocks // INVERSE_GROUP, inverse, 0)
    state_scr[...] = jnp.zeros_like(state_scr)
    gain = gain_ref[...]

    def advance(n, carry):
        q = att_ref[n, 0:128, 0:128]
        k = att_ref[n, 0:128, 128:256]
        cols = cols_scr[n]
        rows = rows_scr[n]
        rk = unit_scale(k, 1.0)
        rq = unit_scale(q, dim**-0.5)
        state = state_scr[...]
        mem_ref[n] = state.astype(BF16)
        recalled = dot_exact_left(jnp.concatenate([k, q], axis=0), state)
        kt = jnp.transpose(k)
        writes = []
        for h in range(2):
            at = slice(128 * h, 128 * (h + 1))
            beta = cols[:, 2 + h : 3 + h]
            rising = cols[:, 4 + h : 5 + h]
            fading = cols[:, 6 + h : 7 + h]
            eks = recalled[0:128, at] * (rk * rising)
            eqs = recalled[128:256, at] * (rq * rising)
            target = att_ref[n, 0:128, 256 + 128 * h : 384 + 128 * h].astype(F32) - eks
            inv = tri_scr[n, :, at]
            score = score_scr[n, :, at]
            update = dot_split(inv, beta * target)
            core = eqs + dot_split(score, update)
            writes.append((rk * fading) * update)
            z = att_ref[n, 0:128, 512 + 128 * h : 640 + 128 * h].astype(F32)
            normed = core * lax.rsqrt(jnp.mean(core * core, axis=-1, keepdims=True) + EPS) * gain
            gated_ref[slot_ref[n], at, :] = jnp.transpose(
                normed * (z * jax.nn.sigmoid(z))
            ).astype(BF16)
            inv_high, inv_low = halves(inv)
            tinv_ref[n, :, at] = inv_high
            tinv_ref[n, :, 256 + 128 * h : 384 + 128 * h] = inv_low
            pair_ref[n, :, at] = score.astype(BF16)
            upd_ref[n, :, at] = update.astype(BF16)
            eks_ref[n, :, at] = eks.astype(BF16)
            eqs_ref[n, :, at] = eqs.astype(BF16)
            core_ref[n, :, at] = core.astype(BF16)
        added = dot_exact_left(kt, jnp.concatenate(writes, axis=1))
        ends = jnp.concatenate(
            [jnp.broadcast_to(rows[4 + h : 5 + h, 127:128], (1, dim)) for h in range(2)], axis=1
        )
        state_scr[...] = ends * state + added
        return carry

    lax.fori_loop(0, blocks, advance, 0)


def backward_kernel(
    order_ref, att_ref, first_ref, last_ref, gain_ref, tinv_ref, pair_ref, upd_ref, eks_ref, eqs_ref, mem_ref, core_ref,
    out_ref,
    rows_scr, cols_scr, dcore_scr, push_scr, dq_state_scr, dtarget_scr, kds_scr, dmem_scr,
    state_scr, colbuf, rowbuf, dgated_ref,
):
    blocks = att_ref.shape[0]
    dim = 128
    logits = vectors(att_ref, rows_scr, cols_scr)
    gain = gain_ref[...]
    for i in range(4):
        dgated_ref[order_ref[i]] = first_ref[i]
        dgated_ref[order_ref[4 + i]] = last_ref[i]
    within = triangle((dim, dim))
    strict = triangle((dim, dim), strict=True)

    def local(n, carry):
        q = att_ref[n, 0:128, 0:128]
        cols = cols_scr[n]
        rq = unit_scale(q, dim**-0.5)
        pushed = []
        for h in range(2):
            at = slice(128 * h, 128 * (h + 1))
            rising = cols[:, 4 + h : 5 + h]
            core = core_ref[n, :, at].astype(F32)
            z = att_ref[n, 0:128, 512 + 128 * h : 640 + 128 * h].astype(F32)
            grad = dgated_ref[n, :, at]
            sigma = jax.nn.sigmoid(z)
            inverse_rms = lax.rsqrt(jnp.mean(core * core, axis=-1, keepdims=True) + EPS)
            normed = core * inverse_rms
            out_ref[n, 0:128, 512 + 128 * h : 640 + 128 * h] = (
                grad * normed * gain * (sigma * (1.0 + z * (1.0 - sigma)))
            ).astype(BF16)
            dnormed = grad * gain * (z * sigma)
            dcore = inverse_rms * (
                dnormed - normed * jnp.mean(dnormed * normed, axis=-1, keepdims=True)
            )
            dcore_scr[n, :, at] = dcore
            push_scr[n, :, at] = dot(pair_ref[n, :, at], dcore.astype(BF16), TN)
            pushed.append((rq * rising) * dcore)
        dq_state_scr[n] = dot(q, jnp.concatenate(pushed, axis=1).astype(BF16), TN)
        return carry

    lax.fori_loop(0, blocks, local, 0)
    state_scr[...] = jnp.zeros_like(state_scr)

    def retreat(i, carry):
        n = blocks - 1 - i
        k = att_ref[n, 0:128, 128:256]
        cols = cols_scr[n]
        rows = rows_scr[n]
        rk = unit_scale(k, 1.0)
        state = state_scr[...]
        dmem_scr[n] = state
        read = dot_exact_left(k, state)
        erased = []
        for h in range(2):
            at = slice(128 * h, 128 * (h + 1))
            beta = cols[:, 2 + h : 3 + h]
            rising = cols[:, 4 + h : 5 + h]
            fading = cols[:, 6 + h : 7 + h]
            kds = read[:, at] * (rk * fading)
            kds_scr[n, :, at] = kds
            high, low = halves(push_scr[n, :, at] + kds)
            inv_high = tinv_ref[n, :, at]
            inv_low = tinv_ref[n, :, 256 + 128 * h : 384 + 128 * h]
            dtarget = dot(
                jnp.concatenate([inv_high, inv_low, inv_high], axis=0),
                jnp.concatenate([high, high, low], axis=0),
                TN,
            )
            dtarget_scr[n, :, at] = dtarget
            erased.append((rk * beta * rising) * dtarget)
        kt = jnp.transpose(k)
        ends = jnp.concatenate(
            [jnp.broadcast_to(rows[4 + h : 5 + h, 127:128], (1, dim)) for h in range(2)], axis=1
        )
        state_scr[...] = (
            ends * state + dq_state_scr[n] - dot_exact_left(kt, jnp.concatenate(erased, axis=1))
        )
        return carry

    lax.fori_loop(0, blocks, retreat, 0)
    last = iota((dim, 1), 0) == dim - 1

    def finish(n, carry):
        q = att_ref[n, 0:128, 0:128]
        k = att_ref[n, 0:128, 128:256]
        cols = cols_scr[n]
        rows = rows_scr[n]
        rk = unit_scale(k, 1.0)
        rq = unit_scale(q, dim**-0.5)
        rk_row = jnp.transpose(jnp.broadcast_to(rk, (dim, dim)))
        both = dot(jnp.concatenate([k, q], axis=0), k, NT)
        kk = both[0:128] * (rk * rk_row)
        qk = both[128:256] * (rq * rk_row)
        dqk = jnp.zeros((dim, dim), F32)
        dkk = jnp.zeros((dim, dim), F32)
        read_out = []
        erase = []
        write = []
        for h in range(2):
            at = slice(128 * h, 128 * (h + 1))
            beta = cols[:, 2 + h : 3 + h]
            rising = cols[:, 4 + h : 5 + h]
            fading = cols[:, 6 + h : 7 + h]
            decay = decay_matrix(cols[:, h : h + 1], rows[h : h + 1, :])
            update = upd_ref[n, :, at]
            dcore = dcore_scr[n, :, at]
            dtarget = dtarget_scr[n, :, at]
            kds = kds_scr[n, :, at]
            outer = dot(
                jnp.concatenate([dcore.astype(BF16), dtarget.astype(BF16)], axis=0), update, NT
            )
            dscore = jnp.where(within, outer[0:128], 0.0) * decay
            dlow = jnp.where(strict, -outer[128:256], 0.0) * decay
            dqk = dqk + dscore
            dkk = dkk + dlow * beta
            dlow_kk = dlow * kk
            eks = eks_ref[n, :, at].astype(F32)
            eqs = eqs_ref[n, :, at].astype(F32)
            value = att_ref[n, 0:128, 256 + 128 * h : 384 + 128 * h].astype(F32)
            out_ref[n, 0:128, 256 + 128 * h : 384 + 128 * h] = (beta * dtarget).astype(BF16)
            dbeta = jnp.sum(dtarget * (value - eks) + dlow_kk, axis=-1, keepdims=True)
            flow = dscore * qk + dlow_kk * beta
            kept = update.astype(F32) * kds
            from_write = jnp.sum(kept, axis=-1, keepdims=True)
            through = jnp.sum(
                mem_ref[n, :, at].astype(F32) * dmem_scr[n, :, at], keepdims=True
            ) * rows[4 + h : 5 + h, 127:128]
            dlog = (
                jnp.sum(flow + dcore * eqs - (beta * dtarget) * eks, axis=-1, keepdims=True)
                - from_write
            )
            dlog = dlog + jnp.where(last, jnp.sum(from_write, keepdims=True) + through, 0.0)
            colbuf[n, :, h : h + 1] = dlog
            colbuf[n, :, 2 + h : 3 + h] = dbeta
            rowbuf[n, h : h + 1, :] = -jnp.sum(flow, axis=0, keepdims=True)
            read_out.append(rising * dcore)
            erase.append((-(beta * rising)) * dtarget)
            write.append(fading * update.astype(F32))
        mem = mem_ref[n]
        top = jnp.concatenate(
            [jnp.concatenate(read_out, axis=1), jnp.concatenate(erase, axis=1)], axis=0
        ).astype(BF16)
        from_mem = dot(top, mem, NT)
        dk = from_mem[128:256] + dot(
            jnp.concatenate(write, axis=1).astype(BF16), dmem_scr[n].astype(BF16), NT
        )
        dq = from_mem[0:128] + dot((dqk * rk_row).astype(BF16), k)
        dk = dk + dot((dqk * rq).astype(BF16), q, TN)
        dk = dk + dot(((dkk + jnp.transpose(dkk)) * rk_row).astype(BF16), k)
        qf = q.astype(F32)
        kf = k.astype(F32)
        dq = rq * (dq - qf * ((rq * rq * dim) * jnp.sum(qf * dq, axis=-1, keepdims=True)))
        dk = rk * (dk - kf * ((rk * rk) * jnp.sum(kf * dk, axis=-1, keepdims=True)))
        out_ref[n, 0:128, 0:128] = dq.astype(BF16)
        out_ref[n, 0:128, 128:256] = dk.astype(BF16)
        return carry

    colbuf[...] = jnp.zeros_like(colbuf)
    rowbuf[...] = jnp.zeros_like(rowbuf)
    lax.fori_loop(0, blocks, finish, 0)
    cols = jnp.concatenate(
        [colbuf[n, :, 0:8] for n in range(blocks)]
        + [jnp.zeros((dim, dim - 8 * blocks), F32)],
        axis=1,
    )
    grads = jnp.transpose(cols)[0 : 8 * blocks] + jnp.concatenate(
        [rowbuf[n] for n in range(blocks)], axis=0
    )
    kind = iota(grads.shape, 0) % 8
    after = mask01(iota((dim, dim), 0) >= iota((dim, dim), 1))
    sigma = jax.nn.sigmoid(logits)
    grads = jnp.where(
        kind < 2, -dot_ones(grads, after) * sigma, grads * sigma * (1.0 - sigma)
    ).astype(BF16)
    for n in range(blocks):
        out_ref[n, 128:136, 0:128] = grads[8 * n : 8 * (n + 1)]
        out_ref[n, 128:136, 128:768] = jnp.zeros((8, 640), BF16)


def sum_kernel(in_ref, out_ref):
    total = jnp.sum(in_ref[...].astype(F32), axis=0)
    out_ref[...] = jnp.transpose(total)


def shape(dims, dtype=BF16):
    return jax.ShapeDtypeStruct(dims, dtype)


def whole(*dims):
    return pl.BlockSpec(dims, lambda *ids: (0,) * len(dims))


def vmem_call(kernel, outs, scratch=(), flops=0, moved=0, limit=56, scalars=0, args=0):
    specs = [pl.BlockSpec(memory_space=pltpu.SMEM)] * scalars
    specs += [pl.BlockSpec(memory_space=pltpu.VMEM)] * args
    return pl.pallas_call(
        kernel,
        in_specs=specs,
        out_shape=outs,
        scratch_shapes=list(scratch),
        compiler_params=params(limit),
        cost_estimate=pl.CostEstimate(flops=flops, bytes_accessed=moved, transcendentals=0),
    )


def run_forward(slot, att, gain):
    blocks = att.shape[0]
    square = (blocks, 128, 256)
    return vmem_call(
        forward_kernel,
        [shape((blocks, 256, 128)), shape((blocks, 128, 512))] + [shape(square)] * 6,
        [
            pltpu.VMEM((blocks, 8, 128), F32),
            pltpu.VMEM((blocks, 128, 128), F32),
            pltpu.VMEM(square, F32),
            pltpu.VMEM(square, F32),
            pltpu.VMEM((128, 256), F32),
        ],
        flops=4 * 10**9,
        moved=8 * MIB,
        scalars=1,
        args=2,
    )(slot, att, gain)


def run_backward(order, att, first, last, gain, saved):
    blocks = att.shape[0]
    square = (blocks, 128, 256)
    return vmem_call(
        backward_kernel,
        shape((blocks, 136, 768)),
        [pltpu.VMEM((blocks, 8, 128), F32), pltpu.VMEM((blocks, 128, 128), F32)]
        + [pltpu.VMEM(square, F32)] * 6
        + [
            pltpu.VMEM((128, 256), F32),
            pltpu.VMEM((blocks, 128, 128), F32),
            pltpu.VMEM((blocks, 8, 128), F32),
            pltpu.VMEM(square, F32),
        ],
        flops=6 * 10**9,
        moved=8 * MIB,
        scalars=1,
        args=4 + len(saved),
    )(order, att, first, last, gain, *saved)


def run_dispatch(hidden, grad, gain, ids, weight, slots):
    tokens, width = hidden.shape
    steps = 4
    return pl.pallas_call(
        dispatch_kernel,
        grid=(steps,),
        in_specs=[
            whole(tokens, width), whole(tokens, width), whole(1, width),
            whole(*ids.shape), whole(*ids.shape),
        ],
        out_specs=pl.BlockSpec((2 * slots, width // steps), lambda i: (0, i)),
        out_shape=shape((2 * slots, width)),
        scratch_shapes=[
            pltpu.VMEM((2 * tokens, width), BF16),
            pltpu.VMEM((2 * slots, 2 * tokens), BF16),
            pltpu.VMEM((2 * slots, 1), F32),
        ],
        compiler_params=params(),
        cost_estimate=pl.CostEstimate(flops=10**9, bytes_accessed=6 * MIB, transcendentals=0),
    )(hidden, grad, gain, ids, weight)


def run_experts(got, gate_up, down):
    rows, width = got.shape
    slots = rows // 2
    hidden_units = down.shape[0]
    return pl.pallas_call(
        expert_kernel,
        in_specs=[
            pl.BlockSpec(memory_space=pltpu.VMEM),
            pl.BlockSpec(memory_space=pl.ANY),
            pl.BlockSpec(memory_space=pl.ANY),
        ],
        out_shape=[
            shape((2 * slots, width // 2)), shape((slots, width)), shape((slots, width)),
            shape((slots, hidden_units)), shape((slots, 2 * hidden_units)),
        ],
        scratch_shapes=[
            pltpu.VMEM((width, 2 * hidden_units), BF16),
            pltpu.VMEM((hidden_units, width), BF16),
            pltpu.SemaphoreType.DMA((2,)),
        ],
        compiler_params=params(),
        cost_estimate=pl.CostEstimate(
            flops=6 * 10**9, bytes_accessed=18 * MIB, transcendentals=0
        ),
    )(got, gate_up, down)


def run_combine(returned, hidden, grad, gain, ids):
    return vmem_call(
        combine_kernel, shape(hidden.shape), flops=10**9, moved=5 * MIB, limit=48, args=5
    )(returned, hidden, grad, gain, ids)


def block_order(me, ctx):
    shift = jnp.array([0, 0, ctx - 2, 2, ctx - 2, 2, 4, 4], jnp.int32)
    flip = jnp.array([0, 1, 0, 0, 1, 1, 0, 1], jnp.int32)
    order = ((me + shift) % ctx) ^ flip
    position = lax.iota(jnp.int32, ctx)
    chip = (position // 2 - me // 2 + ctx // 2) % (ctx // 2)
    other = (position ^ me) & 1
    slot = jnp.where(
        chip == 0, other, jnp.where(chip == 2, 6 + other, jnp.where(chip == 1, 3, 2) + 2 * other)
    )
    return order, slot


def project_hidden(hidden, proj, gated, scale, ctx, exp):
    def send(x, step):
        return lax.ppermute(x, "ctx", [(i, (i + step) % ctx) for i in range(ctx)])

    def swap(x):
        return lax.ppermute(x, "ctx", [(i, i ^ 1) for i in range(ctx)])

    half = hidden.shape[0] // 2
    before = send(hidden, 2)
    after = send(hidden, ctx - 2)
    mate = swap(hidden)
    far = [send(before[:half], 2), send(after[half:], ctx - 2)]
    before_mate = swap(before)
    after_mate = swap(after)
    chunks = (exp, 256, hidden.shape[1] // exp)
    grads = shape((4, 128, 256), F32)
    first, sofar = vmem_call(
        project_first_kernel, [grads, shape(chunks, F32)], flops=10**9, moved=6 * MIB,
        limit=28, args=6,
    )(hidden, mate, before, after, proj, gated)
    far_mate = [swap(x) for x in far]
    last, terms = vmem_call(
        functools.partial(project_last_kernel, scale=scale),
        [grads, shape(chunks)],
        flops=10**9,
        moved=7 * MIB,
        limit=28,
        args=9,
    )(before_mate, after_mate, *far, *far_mate, proj, gated, sofar)
    return first, last, terms


def body(
    hidden_in, grad_out, post_gain, route_ids, route_weight, gate_up, down_proj,
    query_in, key_in, value_in, gate_in, decay_logit, beta_logit, head_gain, out_proj,
):
    ctx = lax.axis_size("ctx")
    exp = lax.axis_size("exp")
    devices = ctx * exp
    order, slot = block_order(lax.axis_index("ctx"), ctx)
    tokens, width = hidden_in.shape[1:]
    slots = 4 * devices
    hidden = hidden_in[0]
    grad = grad_out[0]
    gain = post_gain.reshape(1, width)
    gain_heads = head_gain.reshape(1, 128)
    ids = jnp.transpose(route_ids, (2, 0, 1))

    rows = run_dispatch(
        hidden, grad, gain, ids, jnp.transpose(route_weight, (2, 0, 1)), slots
    )
    got = lax.all_to_all(
        rows.reshape(devices, 8, width), ("ctx", "exp"), split_axis=0, concat_axis=0, tiled=True
    ).reshape(2 * slots, width)
    packed = vmem_call(pack_kernel, shape((ctx, 136, 768)), moved=4 * MIB, limit=12, args=6)(
        query_in[0], key_in[0], value_in[0], gate_in[0], decay_logit[0].T, beta_logit[0].T
    )

    got, packed = lax.optimization_barrier((got, packed))
    att = lax.all_to_all(packed, "ctx", split_axis=0, concat_axis=0, tiled=True)
    back, rows_in, rows_grad, act, gproj = run_experts(got, gate_up[0], down_proj[0])

    back, att = lax.optimization_barrier((back, att))
    returned = lax.all_to_all(
        back.reshape(devices, 8, width // 2), ("ctx", "exp"), split_axis=0, concat_axis=0, tiled=True
    ).reshape(2 * slots, width // 2)
    gated, *saved = run_forward(slot, att, gain_heads)
    grad_gate_up = dot(rows_in, gproj, TN).astype(BF16)
    grad_down = dot(act, rows_grad, TN).astype(BF16)
    returned, gated, saved, grad_gate_up, grad_down = lax.optimization_barrier(
        (returned, gated, saved, grad_gate_up, grad_down)
    )

    grad_hidden = run_combine(returned, hidden, grad, gain, ids)
    scale = float(tokens * devices) ** (-0.5)
    first, last, terms = project_hidden(grad_hidden, out_proj, gated, scale, ctx, exp)
    terms = lax.all_to_all(terms, "exp", split_axis=0, concat_axis=0, tiled=True)

    grads = run_backward(order, att, first, last, gain_heads, saved)
    grads = lax.all_to_all(grads, "ctx", split_axis=0, concat_axis=0, tiled=True)

    grad_out_proj = vmem_call(
        sum_kernel, shape((width // exp, 256), F32), moved=MIB, limit=6, args=1
    )(terms)

    heads = decay_logit.shape[2]
    dq, dk, dv, dz, ddecay, dbeta = vmem_call(
        unpack_kernel,
        [
            shape(query_in.shape[1:]), shape(key_in.shape[1:]), shape(value_in.shape[1:]),
            shape(gate_in.shape[1:]), shape((heads, tokens)), shape((heads, tokens)),
        ],
        moved=4 * MIB,
        limit=12,
        args=1,
    )(grads)
    return (
        grad_hidden[None], dq[None], dk[None], dv[None], dz[None], ddecay.T[None], dbeta.T[None],
        grad_gate_up[None], grad_down[None], grad_out_proj,
    )


def solution(mesh):
    tokens = P("exp", "ctx", None)
    experts = P(("ctx", "exp"), None, None)
    return jax.shard_map(
        body,
        mesh=mesh,
        in_specs=(
            tokens, tokens, P(), tokens, tokens, experts, experts,
            tokens, tokens, tokens, tokens, tokens, tokens, P(), P(None, "ctx"),
        ),
        out_specs=(
            tokens, tokens, tokens, tokens, tokens, tokens, tokens,
            experts, experts, P("exp", "ctx"),
        ),
        check_vma=False,
    )
```
